32 devices in a mesh: ladder: 4 (over y, x), grp: 8 (over z, core).
Axes of the slice: x: 2, y: 2, z: 4, core: 2. Of those that a mesh axis runs over, the one named last changes fastest.
Arguments:
- init_up: int32 [512, 144], P(('ladder', 'grp')), may hold values 0 or 1
- flip_site: int32 [4, 512], P(None, ('ladder', 'grp')), may hold values from 0 to 143
- accept: int32 [4, 512], P(None, ('ladder', 'grp')), may hold values from 0 to 1
- swap_ok: int32 [4, 2, 128], P(None, None, 'grp'), may hold values 0 or 1
- ladder_bit: int32 [4, 8], P(None, 'grp'), may hold values from 0 to 1
- w_embed: bfloat16 [4, 72], replicated, may hold values from -3 to 3
- pos_embed: float32 [36, 72], replicated, may hold values from -6 to 6
- w_value: bfloat16 [2, 72, 72], replicated, may hold values from -0.75 to 0.75
- mixing: float32 [2, 12, 36, 36], replicated, may hold values from -1 to 1
- w_out: bfloat16 [2, 72, 72], replicated, may hold values from -0.75 to 0.75
- w_in: bfloat16 [2, 72, 288], replicated, may hold values from -0.75 to 0.75
- w_back: bfloat16 [2, 288, 72], replicated, may hold values from -0.375 to 0.375
- w_final: float32 [72, 72], replicated, may hold values from -0.75 to 0.75
- b_final: float32 [72], replicated, may hold values from -5 to 5
Outputs:
- proposal_amp: float32 [4, 512], P(None, ('ladder', 'grp'))
- final_spins: float32 [512, 144], P(('ladder', 'grp'))
- final_amp: float32 [512], P(('ladder', 'grp'))
- accept_counts: float32 [4, 4], P('ladder')
The draws below stay inside these ranges and needn't reach their ends.
All inputs are finite; a program needn't handle non-finite values. No bound on the sum of `init_up` or of `swap_ok` on one device may be relied on, other than what follows from the above.
Results may differ from the reference program's by a relative error of at most 0.002.
Values sent between devices are 32-bit elements; how exact they have to be, the bound alone decides.
A program may use at most 64 MiB of HBM per device.

```python
import jax
import jax.numpy as jnp
from jax import lax

SIDE = 12
SITES = 144
PATCHES = 36
D = 72
HEADS = 12
HID = 288
LAYERS = 2
STEPS = 4
CHAINS_RUNG = 128
CHAINS = 512
LADDER_BITS = 2
PAIRS = 2
N_LADDER = 4
N_GRP = 8


def draw_accept(key, part):
    chain_index = lax.broadcasted_iota(jnp.int32, (STEPS, CHAINS), 1) % CHAINS_RUNG
    threshold = 200 + 400 * chain_index // CHAINS_RUNG
    tickets = jax.random.randint(jax.random.fold_in(key, 11), (STEPS, CHAINS), 0, 1000)
    return (tickets < threshold).astype(jnp.int32)


def plant(entries, rng, low, largest):
    longest = entries.shape.index(max(entries.shape))
    spots = []
    for shift in (0, 1):
        where = [jax.random.randint(jax.random.fold_in(rng, axis), (), 0, length) for axis, length in enumerate(entries.shape)]
        where[longest] = (where[longest] + shift) % entries.shape[longest]
        spots.append(tuple(where))
    return entries.at[spots[0]].set(low).at[spots[1]].set(largest)


def noise(rng, dims, scale, limit, held_as=jnp.bfloat16):
    values = jax.random.normal(rng, dims, jnp.float32) * scale
    return jnp.minimum(jnp.maximum(values, -limit), limit).astype(held_as)


def setup_inputs(seed: int = 0) -> dict:
    arg_keys = jax.random.split(jax.random.key(seed), 15)
    init_up = plant((jax.random.randint(arg_keys[0], (CHAINS, SITES), 0, 2) < 1).astype(jnp.int32), jax.random.fold_in(arg_keys[0], 1), 0, 1)
    flip_site = plant(jax.random.randint(arg_keys[1], (STEPS, CHAINS), 0, SITES), jax.random.fold_in(arg_keys[1], 1), 0, SITES - 1).astype(jnp.int32)
    accept = draw_accept(jax.random.fold_in(arg_keys[14], 71), 0)
    swap_ok = plant((jax.random.randint(arg_keys[3], (STEPS, PAIRS, CHAINS_RUNG), 0, 2) < 1).astype(jnp.int32), jax.random.fold_in(arg_keys[3], 1), 0, 1)
    ladder_bit = plant(jax.random.randint(arg_keys[4], (STEPS, N_GRP), 0, LADDER_BITS), jax.random.fold_in(arg_keys[4], 1), 0, LADDER_BITS - 1).astype(jnp.int32)
    w_embed = noise(arg_keys[5], (4, D), 4 ** -0.5, 3.0)
    pos_embed = noise(arg_keys[6], (PATCHES, D), 1.0, 6.0, jnp.float32)
    w_value = noise(arg_keys[7], (LAYERS, D, D), D ** -0.5, 0.75)
    mixing = noise(arg_keys[8], (LAYERS, HEADS, PATCHES, PATCHES), PATCHES ** -0.5, 1.0, jnp.float32)
    w_out = noise(arg_keys[9], (LAYERS, D, D), D ** -0.5, 0.75)
    w_in = noise(arg_keys[10], (LAYERS, D, HID), D ** -0.5, 0.75)
    w_back = noise(arg_keys[11], (LAYERS, HID, D), HID ** -0.5, 0.375)
    w_final = noise(arg_keys[12], (D, D), D ** -0.5, 0.75, jnp.float32)
    b_final = noise(arg_keys[13], (D,), 1.0, 5.0, jnp.float32)
    return {"init_up": init_up, "flip_site": flip_site, "accept": accept, "swap_ok": swap_ok, "ladder_bit": ladder_bit, "w_embed": w_embed, "pos_embed": pos_embed, "w_value": w_value, "mixing": mixing, "w_out": w_out, "w_in": w_in, "w_back": w_back, "w_final": w_final, "b_final": b_final}


def layer_norm(values):
    center = values - lax.optimization_barrier(jnp.mean(values, axis=-1, keepdims=True))
    spread = lax.optimization_barrier(jnp.mean(center * center, axis=-1, keepdims=True))
    return center / jnp.sqrt(spread + 1e-05)

def log_cosh(values):
    return jnp.logaddexp(values, -values) - jnp.log(2.0)

def amplitude(spin_state, w_embed, pos_embed, w_value, mixing, w_out, w_in, w_back, w_final, b_final):
    chains = spin_state.shape[0]
    half_side = SIDE // 2
    patch_count = half_side * half_side
    patches = spin_state.reshape(chains, half_side, 2, half_side, 2).transpose(0, 1, 3, 2, 4).reshape(chains * patch_count, 4)
    stream = jnp.dot(patches, w_embed.astype(jnp.float32), precision=lax.Precision.HIGHEST)
    model_width = stream.shape[-1]
    stream = stream.reshape(chains, patch_count, model_width) + pos_embed
    head_count = mixing.shape[1]
    row_count = chains * patch_count
    for layer_index in range(w_value.shape[0]):
        normed = layer_norm(stream).astype(jnp.bfloat16).reshape(row_count, model_width)
        value_rows = jnp.dot(normed, w_value[layer_index], preferred_element_type=jnp.float32).astype(jnp.bfloat16)
        value_rows = value_rows.astype(jnp.float32).reshape(chains, patch_count, head_count, model_width // head_count)
        mixed_heads = jnp.einsum('hpq,nqhd->nphd', mixing[layer_index], value_rows, precision=lax.Precision.HIGHEST)
        mixed_heads = mixed_heads.astype(jnp.bfloat16).reshape(row_count, model_width)
        attended = jnp.dot(mixed_heads, w_out[layer_index], preferred_element_type=jnp.float32)
        stream = stream + attended.reshape(chains, patch_count, model_width)
        normed = layer_norm(stream).astype(jnp.bfloat16).reshape(row_count, model_width)
        hidden = jax.nn.gelu(jnp.dot(normed, w_in[layer_index], preferred_element_type=jnp.float32)).astype(jnp.bfloat16)
        backed = jnp.dot(hidden, w_back[layer_index], preferred_element_type=jnp.float32)
        stream = stream + backed.reshape(chains, patch_count, model_width)
    pooled = lax.optimization_barrier(jnp.sum(layer_norm(stream), axis=1)) / half_side
    head_values = jnp.dot(pooled, w_final, precision=lax.Precision.HIGHEST) + b_final
    return lax.optimization_barrier(jnp.mean(log_cosh(head_values), axis=-1))

def flipped(spin_state, sites):
    columns = lax.broadcasted_iota(jnp.int32, spin_state.shape, 1)
    return jnp.where(columns == sites[:, None].astype(jnp.int32), -spin_state, spin_state)

def reference(init_up, flip_site, accept, swap_ok, ladder_bit, w_embed, pos_embed, w_value, mixing, w_out, w_in, w_back, w_final, b_final):
    params = (w_embed, pos_embed, w_value, mixing, w_out, w_in, w_back, w_final, b_final)

    def rung_amplitudes(spin_state):
        blocks = spin_state.reshape(N_LADDER, CHAINS_RUNG, SITES)
        return lax.map(lambda rung_block: amplitude(rung_block, *params), blocks).reshape(CHAINS)
    spin_state = 2.0 * init_up.astype(jnp.float32) - 1.0
    log_amp = rung_amplitudes(spin_state)
    rungs = jnp.arange(N_LADDER, dtype=jnp.int32)
    per_block = CHAINS_RUNG // N_GRP
    proposals = []
    for step_index in range(STEPS):
        proposal = flipped(spin_state, flip_site[step_index])
        proposal_amp = rung_amplitudes(proposal)
        proposals.append(proposal_amp)
        taken = accept[step_index] == 1
        spin_state = jnp.where(taken[:, None], proposal, spin_state)
        log_amp = jnp.where(taken, proposal_amp, log_amp)
        block_stride = jnp.left_shift(jnp.int32(1), ladder_bit[step_index].astype(jnp.int32))
        place_stride = jnp.repeat(block_stride, per_block).astype(jnp.int32)
        partner = jnp.bitwise_xor(rungs[:, None], place_stride[None, :]).astype(jnp.int32)
        lower = jnp.minimum(rungs[:, None], partner)
        pair_index = (lower // (2 * place_stride[None, :]) * place_stride[None, :] + lower % place_stride[None, :]).astype(jnp.int32)
        decided = jnp.take_along_axis(swap_ok[step_index], pair_index, axis=0) == 1
        grouped = spin_state.reshape(N_LADDER, CHAINS_RUNG, SITES)
        partner_spins = jnp.take_along_axis(grouped, partner[:, :, None], axis=0)
        spin_state = jnp.where(decided[:, :, None], partner_spins, grouped).reshape(CHAINS, SITES)
        amp_grouped = log_amp.reshape(N_LADDER, CHAINS_RUNG)
        partner_amp = jnp.take_along_axis(amp_grouped, partner, axis=0)
        log_amp = jnp.where(decided, partner_amp, amp_grouped).reshape(CHAINS)
    counts = lax.optimization_barrier(jnp.sum(accept.reshape(STEPS, N_LADDER, CHAINS_RUNG), axis=2)).T.astype(jnp.float32)
    return (jnp.stack(proposals), spin_state, log_amp, counts)
```

```python
import functools
import math

import jax
import jax.numpy as jnp
from jax import lax
from jax.experimental import pallas as pl
from jax.experimental.pallas import tpu as pltpu
from jax.sharding import PartitionSpec as P

MESH = pl.DeviceIdType.MESH
VMEM = pltpu.VMEM
F32 = jnp.float32
BF16 = jnp.bfloat16


def exchange_kernel(
    rungs, groups, up_ref, flip_ref, accept_ref, ups_ref, flips_ref, accepts_ref, counts_ref,
    send_sem, recv_sem, group_send, group_recv,
):
    rung = lax.axis_index("ladder")
    place = lax.axis_index("grp")
    barrier = pltpu.get_barrier_semaphore()
    for apart in range(1, rungs):
        pl.semaphore_signal(
            barrier, inc=1, device_id=(jnp.bitwise_xor(rung, apart), place), device_id_type=MESH
        )
    for apart in range(1, groups):
        pl.semaphore_signal(
            barrier, inc=1, device_id=(rung, jnp.bitwise_xor(place, apart)), device_id_type=MESH
        )
    pl.semaphore_wait(barrier, rungs - 1 + groups - 1)
    copies = []
    for apart in range(1, rungs):
        target = (jnp.bitwise_xor(rung, apart), place)
        for part, (source, landing) in enumerate(
            ((up_ref, ups_ref), (flip_ref, flips_ref), (accept_ref, accepts_ref))
        ):
            copies.append(
                pltpu.make_async_remote_copy(
                    src_ref=source,
                    dst_ref=landing.at[apart - 1],
                    send_sem=send_sem.at[apart - 1, part],
                    recv_sem=recv_sem.at[apart - 1, part],
                    device_id=target,
                    device_id_type=MESH,
                )
            )
            copies[-1].start()
    for apart in range(1, groups):
        copies.append(
            pltpu.make_async_remote_copy(
                src_ref=accept_ref,
                dst_ref=counts_ref.at[apart - 1],
                send_sem=group_send.at[apart - 1],
                recv_sem=group_recv.at[apart - 1],
                device_id=(rung, jnp.bitwise_xor(place, apart)),
                device_id_type=MESH,
            )
        )
        copies[-1].start()
    for copy in copies:
        copy.wait()


def exchange(init_up, flip_site, accept, rungs, groups):
    return pl.pallas_call(
        functools.partial(exchange_kernel, rungs, groups),
        out_shape=(
            jax.ShapeDtypeStruct((rungs - 1,) + init_up.shape, jnp.int32),
            jax.ShapeDtypeStruct((rungs - 1,) + flip_site.shape, jnp.int32),
            jax.ShapeDtypeStruct((rungs - 1,) + accept.shape, jnp.int32),
            jax.ShapeDtypeStruct((groups - 1,) + accept.shape, jnp.int32),
        ),
        in_specs=[pl.BlockSpec(memory_space=VMEM)] * 3,
        out_specs=[pl.BlockSpec(memory_space=VMEM)] * 4,
        scratch_shapes=[
            pltpu.SemaphoreType.DMA((rungs - 1, 3)),
            pltpu.SemaphoreType.DMA((rungs - 1, 3)),
            pltpu.SemaphoreType.DMA((groups - 1,)),
            pltpu.SemaphoreType.DMA((groups - 1,)),
        ],
        compiler_params=pltpu.CompilerParams(collective_id=0, has_side_effects=True),
        name="exchange",
    )(init_up, flip_site, accept)


def transposed(matrix):
    wide = matrix.shape[1]
    eye = (
        lax.broadcasted_iota(jnp.int32, (wide, wide), 0)
        == lax.broadcasted_iota(jnp.int32, (wide, wide), 1)
    )
    return lax.dot_general(
        eye.astype(F32).astype(matrix.dtype),
        matrix,
        (((1,), (1,)), ((), ())),
        preferred_element_type=F32,
    )


def layer_norm(values):
    scale = 1.0 / values.shape[0]
    center = values - jnp.sum(values, axis=0, keepdims=True) * scale
    spread = jnp.sum(center * center, axis=0, keepdims=True) * scale
    return center * lax.rsqrt(spread + 1e-05)


def gelu(values):
    root = math.sqrt(2.0 / math.pi)
    half = 0.5 * values
    inner = values * (root + (root * 0.044715) * (values * values))
    return half + half * jnp.tanh(inner)


def window_kernel(
    up_ref, flip_ref, accept_ref, ups_ref, flips_ref, accepts_ref, counts_ref,
    swap_ref, bit_ref, w_embed_ref, pos_ref, w_value_ref, mixing_ref, w_out_ref, w_in_ref,
    w_back_ref, w_final_ref, b_final_ref,
    proposal_ref, spins_out_ref, amp_ref, totals_ref,
    event_ref, spin_ref, x_ref, v_ref, embed_ref, wv_ref, wo_ref, wi_ref, wb_ref, pool_ref,
):
    chains, sites = up_ref.shape
    steps = flip_ref.shape[0]
    rungs = ups_ref.shape[0] + 1
    bits = rungs.bit_length() - 1
    patch_count, width = pos_ref.shape
    layers, heads = mixing_ref.shape[:2]
    per_head = width // heads
    hidden_width = w_in_ref.shape[2]
    lanes = event_ref.shape[1]
    side = math.isqrt(sites)
    half_side = side // 2
    rung = lax.axis_index("ladder")

    accepted = accept_ref[...]
    total = accepted + jnp.sum(counts_ref[...], axis=0)
    totals_ref[...] = jnp.sum(total.astype(F32), axis=1, keepdims=True)

    rows = event_ref.shape[0]
    row = lax.broadcasted_iota(jnp.int32, (rows, chains), 0)
    state = [jnp.where(row == 0, apart, -1) for apart in range(rungs)]
    event_ref[...] = jnp.full(event_ref.shape, -1, jnp.int32)
    for step in range(steps):
        mine = slice(step, step + 1)
        moved = []
        for apart in range(rungs):
            sites_here = flip_ref[mine, :] if apart == 0 else flips_ref[apart - 1, mine, :]
            taken = accept_ref[mine, :] if apart == 0 else accepts_ref[apart - 1, mine, :]
            if apart == 0:
                event_ref[:, step * chains : (step + 1) * chains] = jnp.where(
                    row == step + 1, sites_here, state[0]
                )
            moved.append(
                jnp.where(row == step + 1, jnp.where(taken == 1, sites_here, -1), state[apart])
            )
        chosen = bit_ref[mine, :]
        after = []
        for apart in range(rungs):
            here = jnp.bitwise_xor(rung, apart)
            value = moved[apart]
            for bit in range(bits):
                mask = 2**bit
                pair = (here // (2 * mask)) * mask + lax.rem(here, mask)
                decided = jnp.where(chosen == bit, swap_ref[step, pl.ds(pair, 1), :], 0)
                value = jnp.where(
                    jnp.broadcast_to(decided, value.shape) == 1, moved[apart ^ mask], value
                )
            after.append(value)
        state = after
    event_ref[:, steps * chains : (steps + 1) * chains] = state[0]

    events = event_ref[...]
    lane = lax.broadcasted_iota(jnp.int32, (1, lanes), 1)
    wanted = events[0:1, :] * chains + lax.rem(lane, chains)
    member = lax.broadcasted_iota(jnp.int32, (rungs * chains, lanes), 0)
    pick = (member == wanted).astype(F32).astype(BF16)
    everyone = jnp.concatenate(
        [up_ref[...], ups_ref[...].reshape((rungs - 1) * chains, sites)], axis=0
    )
    picked = lax.dot_general(
        everyone.astype(F32).astype(BF16), pick, (((0,), (0,)), ((), ())),
        preferred_element_type=F32,
    )
    spins = 2.0 * picked - 1.0
    site = lax.broadcasted_iota(jnp.int32, (sites, lanes), 0)
    for step in range(steps):
        spins = jnp.where(site == events[step + 1 : step + 2, :], -spins, spins)
    spin_ref[...] = spins
    last = (
        lax.broadcasted_iota(jnp.int32, (chains, lanes), 1)
        == lax.broadcasted_iota(jnp.int32, (chains, lanes), 0) + steps * chains
    )
    spins_out_ref[...] = lax.dot_general(
        last.astype(F32).astype(BF16), spins.astype(BF16), (((1,), (1,)), ((), ())),
        preferred_element_type=F32,
    )

    depth = embed_ref.shape[1]
    part_rows = (depth - 8) // 3
    pos = pos_ref[...]
    high = pos.astype(BF16)
    middle = (pos - high.astype(F32)).astype(BF16)
    low = (pos - high.astype(F32) - middle.astype(F32)).astype(BF16)
    blank = jnp.zeros((part_rows - patch_count, width), F32)
    pieces = [w_embed_ref[...].astype(F32), jnp.zeros((8 - w_embed_ref.shape[0], width), F32)]
    for part in (high, middle, low):
        pieces += [part.astype(F32), blank]
    embed_ref[...] = transposed(jnp.concatenate(pieces, axis=0).astype(BF16)).astype(BF16)
    for layer in range(layers):
        wv_ref[layer] = transposed(w_value_ref[layer]).astype(BF16)
        wo_ref[layer] = transposed(w_out_ref[layer]).astype(BF16)
        wi_ref[layer] = transposed(w_in_ref[layer]).astype(BF16)
        wb_ref[layer] = transposed(w_back_ref[layer]).astype(BF16)

    def rows_of(patch):
        return pl.ds(pl.multiple_of(patch * width, 8), width)

    def pair_of(ref, first):
        return jnp.concatenate([ref[rows_of(first), :], ref[rows_of(first + 1), :]], axis=1)

    def put_pair(ref, first, value):
        ref[rows_of(first), :] = value[:, :lanes]
        ref[rows_of(first + 1), :] = value[:, lanes:]

    def matmul(left, right):
        return jnp.dot(left, right, preferred_element_type=F32)

    slot = lax.broadcasted_iota(jnp.int32, (depth, lanes), 0)
    spot = jnp.where(slot < 8, -1, lax.rem(slot + (part_rows - 8), part_rows))
    eight = lax.broadcasted_iota(jnp.int32, (8, lanes), 0)

    def embed_input(patch):
        top = (patch // half_side) * (2 * side) + lax.rem(patch, half_side) * 2
        block = jnp.zeros((8, lanes), F32)
        for index, offset in enumerate((0, 1, side, side + 1)):
            block = jnp.where(eight == index, spin_ref[pl.ds(top + offset, 1), :], block)
        onehot = (spot == patch).astype(F32)
        return jnp.concatenate([block, onehot[8:]], axis=0).astype(BF16)

    def start(pair, carry):
        first = pair * 2
        right = jnp.concatenate([embed_input(first), embed_input(first + 1)], axis=1)
        stream = matmul(embed_ref[...], right)
        put_pair(x_ref, first, stream)
        put_pair(v_ref, first, matmul(wv_ref[0], layer_norm(stream).astype(BF16)))
        return carry

    lax.fori_loop(0, patch_count // 2, start, 0)
    pool_ref[...] = jnp.zeros(pool_ref.shape, F32)

    for layer in range(layers):
        for head in range(heads):
            places = [
                pl.ds(head * per_head + index, patch_count, stride=width)
                for index in range(per_head)
            ]
            value = jnp.concatenate([v_ref[spot_rows, :] for spot_rows in places], axis=1)
            mixed = matmul(mixing_ref[layer, head].astype(BF16), value.astype(BF16))
            for index, spot_rows in enumerate(places):
                v_ref[spot_rows, :] = mixed[:, index * lanes : (index + 1) * lanes]

        def block(pair, carry, layer=layer):
            first = pair * 2
            stream = pair_of(x_ref, first) + matmul(
                wo_ref[layer], pair_of(v_ref, first).astype(BF16)
            )
            normed = layer_norm(stream).astype(BF16)
            hidden = gelu(matmul(wi_ref[layer], normed)).astype(BF16)
            stream = stream + matmul(wb_ref[layer], hidden)
            normed = layer_norm(stream)
            if layer + 1 < layers:
                put_pair(x_ref, first, stream)
                put_pair(v_ref, first, matmul(wv_ref[layer + 1], normed.astype(BF16)))
            else:
                pool_ref[...] += normed[:, :lanes] + normed[:, lanes:]
            return carry

        lax.fori_loop(0, patch_count // 2, block, 0)

    pooled = pool_ref[...] / half_side
    bias = jnp.transpose(jnp.broadcast_to(b_final_ref[...], (lanes, width)))
    final = lax.dot_general(
        w_final_ref[...], pooled, (((0,), (0,)), ((), ())),
        preferred_element_type=F32, precision=lax.Precision.HIGHEST,
    ) + bias
    size = jnp.abs(final)
    curve = size + jnp.log1p(jnp.exp(-2.0 * size)) - math.log(2.0)
    amps = jnp.sum(curve, axis=0, keepdims=True) * (1.0 / width)
    for step in range(steps):
        proposal_ref[step : step + 1, :] = amps[:, step * chains : (step + 1) * chains]
    amp_ref[...] = amps[:, steps * chains : (steps + 1) * chains]


def on_device(
    init_up, flip_site, accept, swap_ok, ladder_bit, w_embed, pos_embed, w_value, mixing, w_out,
    w_in, w_back, w_final, b_final,
):
    rungs, groups = lax.axis_size("ladder"), lax.axis_size("grp")
    chains, sites = init_up.shape
    steps = flip_site.shape[0]
    patch_count, width = pos_embed.shape
    layers, hidden_width = w_in.shape[0], w_in.shape[2]
    ups, flips, accepts, counts = exchange(init_up, flip_site, accept, rungs, groups)
    lanes = -(-(steps + 1) * chains // 128) * 128
    rows = -(-(steps + 1) // 8) * 8
    depth = 8 + 3 * (-(-patch_count // 8) * 8)
    proposals, spins, amp, totals = pl.pallas_call(
        window_kernel,
        out_shape=(
            jax.ShapeDtypeStruct((steps, chains), F32),
            jax.ShapeDtypeStruct((chains, sites), F32),
            jax.ShapeDtypeStruct((1, chains), F32),
            jax.ShapeDtypeStruct((steps, 1), F32),
        ),
        in_specs=[pl.BlockSpec(memory_space=VMEM)] * 18,
        out_specs=[pl.BlockSpec(memory_space=VMEM)] * 4,
        scratch_shapes=[
            VMEM((rows, lanes), jnp.int32),
            VMEM((sites, lanes), F32),
            VMEM((patch_count * width, lanes), F32),
            VMEM((patch_count * width, lanes), F32),
            VMEM((width, depth), BF16),
            VMEM((layers, width, width), BF16),
            VMEM((layers, width, width), BF16),
            VMEM((layers, hidden_width, width), BF16),
            VMEM((layers, width, hidden_width), BF16),
            VMEM((width, lanes), F32),
        ],
        name="window",
    )(
        init_up, flip_site, accept, ups, flips, accepts, counts, swap_ok, ladder_bit, w_embed,
        pos_embed, w_value, mixing, w_out, w_in, w_back, w_final, b_final.reshape(1, width),
    )
    return proposals, spins, amp.reshape(chains), totals.reshape(1, steps)


def solution(mesh):
    placed = (
        P(("ladder", "grp"), None),
        P(None, ("ladder", "grp")),
        P(None, ("ladder", "grp")),
        P(None, None, "grp"),
        P(None, "grp"),
    ) + (P(),) * 9
    return jax.shard_map(
        on_device,
        mesh=mesh,
        in_specs=placed,
        out_specs=(
            P(None, ("ladder", "grp")),
            P(("ladder", "grp"), None),
            P(("ladder", "grp")),
            P("ladder", None),
        ),
        check_vma=False,
    )
```

```python
import functools
import math

import jax
import jax.numpy as jnp
from jax import lax
from jax.experimental import pallas as pl
from jax.experimental.pallas import tpu as pltpu
from jax.sharding import PartitionSpec as P

MESH = pl.DeviceIdType.MESH
VMEM = pltpu.VMEM
F32 = jnp.float32
BF16 = jnp.bfloat16
GROUP = 9


def exchange_kernel(
    rungs, groups, up_ref, flip_ref, accept_ref, ups_ref, flips_ref, accepts_ref, counts_ref,
    send_sem, recv_sem, group_send, group_recv,
):
    rung = lax.axis_index("ladder")
    place = lax.axis_index("grp")
    barrier = pltpu.get_barrier_semaphore()
    for apart in range(1, rungs):
        pl.semaphore_signal(
            barrier, inc=1, device_id=(jnp.bitwise_xor(rung, apart), place), device_id_type=MESH
        )
    for apart in range(1, groups):
        pl.semaphore_signal(
            barrier, inc=1, device_id=(rung, jnp.bitwise_xor(place, apart)), device_id_type=MESH
        )
    pl.semaphore_wait(barrier, rungs - 1 + groups - 1)
    copies = []
    for apart in range(1, rungs):
        target = (jnp.bitwise_xor(rung, apart), place)
        for part, (source, landing) in enumerate(
            ((up_ref, ups_ref), (flip_ref, flips_ref), (accept_ref, accepts_ref))
        ):
            copies.append(
                pltpu.make_async_remote_copy(
                    src_ref=source,
                    dst_ref=landing.at[apart - 1],
                    send_sem=send_sem.at[apart - 1, part],
                    recv_sem=recv_sem.at[apart - 1, part],
                    device_id=target,
                    device_id_type=MESH,
                )
            )
            copies[-1].start()
    for apart in range(1, groups):
        copies.append(
            pltpu.make_async_remote_copy(
                src_ref=accept_ref,
                dst_ref=counts_ref.at[apart - 1],
                send_sem=group_send.at[apart - 1],
                recv_sem=group_recv.at[apart - 1],
                device_id=(rung, jnp.bitwise_xor(place, apart)),
                device_id_type=MESH,
            )
        )
        copies[-1].start()
    for copy in copies:
        copy.wait()


def exchange(init_up, flip_site, accept, rungs, groups):
    return pl.pallas_call(
        functools.partial(exchange_kernel, rungs, groups),
        out_shape=(
            jax.ShapeDtypeStruct((rungs - 1,) + init_up.shape, jnp.int32),
            jax.ShapeDtypeStruct((rungs - 1,) + flip_site.shape, jnp.int32),
            jax.ShapeDtypeStruct((rungs - 1,) + accept.shape, jnp.int32),
            jax.ShapeDtypeStruct((groups - 1,) + accept.shape, jnp.int32),
        ),
        in_specs=[pl.BlockSpec(memory_space=VMEM)] * 3,
        out_specs=[pl.BlockSpec(memory_space=VMEM)] * 4,
        scratch_shapes=[
            pltpu.SemaphoreType.DMA((rungs - 1, 3)),
            pltpu.SemaphoreType.DMA((rungs - 1, 3)),
            pltpu.SemaphoreType.DMA((groups - 1,)),
            pltpu.SemaphoreType.DMA((groups - 1,)),
        ],
        compiler_params=pltpu.CompilerParams(collective_id=0, has_side_effects=True),
        name="exchange",
    )(init_up, flip_site, accept)


def transposed(matrix):
    wide = matrix.shape[1]
    eye = (
        lax.broadcasted_iota(jnp.int32, (wide, wide), 0)
        == lax.broadcasted_iota(jnp.int32, (wide, wide), 1)
    )
    return lax.dot_general(
        eye.astype(F32).astype(matrix.dtype),
        matrix,
        (((1,), (1,)), ((), ())),
        preferred_element_type=F32,
    )


def layer_norm(values):
    scale = 1.0 / values.shape[0]
    center = values - jnp.sum(values, axis=0, keepdims=True) * scale
    spread = jnp.sum(center * center, axis=0, keepdims=True) * scale
    return center * lax.rsqrt(spread + 1e-05)


def twice_gelu(values):
    root = math.sqrt(2.0 / math.pi)
    inner = values * (root + (root * 0.044715) * (values * values))
    return values + values * jnp.tanh(inner)


def window_kernel(
    up_ref, flip_ref, accept_ref, ups_ref, flips_ref, accepts_ref, counts_ref,
    swap_ref, bit_ref, w_embed_ref, pos_ref, w_value_ref, mixing_ref, w_out_ref, w_in_ref,
    w_back_ref, w_final_ref, b_final_ref,
    proposal_ref, spins_out_ref, amp_ref, totals_ref,
    event_ref, spin_ref, x_ref, v_ref, embed_ref, wv_ref, wo_ref, wi_ref, wb_ref, pool_ref,
):
    chains, sites = up_ref.shape
    steps = flip_ref.shape[0]
    rungs = ups_ref.shape[0] + 1
    bits = rungs.bit_length() - 1
    patch_count, width = pos_ref.shape
    layers = w_value_ref.shape[0]
    heads = mixing_ref.shape[0] // (layers * patch_count)
    per_head = width // heads
    hidden_width = w_in_ref.shape[2]
    lanes = event_ref.shape[1]
    side = math.isqrt(sites)
    half_side = side // 2
    rung = lax.axis_index("ladder")

    accepted = accept_ref[...]
    total = accepted + jnp.sum(counts_ref[...], axis=0)
    totals_ref[...] = lax.dot_general(
        jnp.ones((1, chains), F32), total.astype(F32), (((1,), (1,)), ((), ())),
        preferred_element_type=F32, precision=lax.Precision.HIGHEST,
    )

    rows = event_ref.shape[0]
    row = lax.broadcasted_iota(jnp.int32, (rows, chains), 0)
    state = [jnp.where(row == 0, apart, -1) for apart in range(rungs)]
    event_ref[...] = jnp.full(event_ref.shape, -1, jnp.int32)
    for step in range(steps):
        mine = slice(step, step + 1)
        moved = []
        for apart in range(rungs):
            sites_here = flip_ref[mine, :] if apart == 0 else flips_ref[apart - 1, mine, :]
            taken = accept_ref[mine, :] if apart == 0 else accepts_ref[apart - 1, mine, :]
            if apart == 0:
                event_ref[:, step * chains : (step + 1) * chains] = jnp.where(
                    row == step + 1, sites_here, state[0]
                )
            moved.append(
                jnp.where(row == step + 1, jnp.where(taken == 1, sites_here, -1), state[apart])
            )
        chosen = bit_ref[:, mine]
        after = []
        for apart in range(rungs):
            here = jnp.bitwise_xor(rung, apart)
            value = moved[apart]
            for bit in range(bits):
                mask = 2**bit
                pair = (here // (2 * mask)) * mask + lax.rem(here, mask)
                decided = jnp.where(chosen == bit, swap_ref[step, pl.ds(pair, 1), :], 0)
                value = jnp.where(
                    jnp.broadcast_to(decided, value.shape) == 1, moved[apart ^ mask], value
                )
            after.append(value)
        state = after
    event_ref[:, steps * chains : (steps + 1) * chains] = state[0]

    events = event_ref[...]
    lane = lax.broadcasted_iota(jnp.int32, (1, lanes), 1)
    wanted = events[0:1, :] * chains + lax.rem(lane, chains)
    member = lax.broadcasted_iota(jnp.int32, (rungs * chains, lanes), 0)
    pick = (member == wanted).astype(F32).astype(BF16)
    everyone = jnp.concatenate(
        [up_ref[...], ups_ref[...].reshape((rungs - 1) * chains, sites)], axis=0
    )
    picked = lax.dot_general(
        everyone.astype(F32).astype(BF16), pick, (((0,), (0,)), ((), ())),
        preferred_element_type=F32,
    )
    spins = 2.0 * picked - 1.0
    site = lax.broadcasted_iota(jnp.int32, (sites, lanes), 0)
    for step in range(steps):
        spins = jnp.where(site == events[step + 1 : step + 2, :], -spins, spins)
    spin_ref[...] = spins
    last = (
        lax.broadcasted_iota(jnp.int32, (chains, lanes), 1)
        == lax.broadcasted_iota(jnp.int32, (chains, lanes), 0) + steps * chains
    )
    spins_out_ref[...] = lax.dot_general(
        last.astype(F32).astype(BF16), spins.astype(BF16), (((1,), (1,)), ((), ())),
        preferred_element_type=F32,
    )

    depth = embed_ref.shape[1]
    part_rows = (depth - 8) // 3
    pos = pos_ref[...]
    high = pos.astype(BF16)
    middle = (pos - high.astype(F32)).astype(BF16)
    low = (pos - high.astype(F32) - middle.astype(F32)).astype(BF16)
    blank = jnp.zeros((part_rows - patch_count, width), F32)
    pieces = [w_embed_ref[...].astype(F32), jnp.zeros((8 - w_embed_ref.shape[0], width), F32)]
    for part in (high, middle, low):
        pieces += [part.astype(F32), blank]
    embed_ref[...] = transposed(jnp.concatenate(pieces, axis=0).astype(BF16)).astype(BF16)
    for layer in range(layers):
        wv_ref[layer] = transposed(w_value_ref[layer]).astype(BF16)
        wo_ref[layer] = transposed(w_out_ref[layer]).astype(BF16)
        wi_ref[layer] = transposed(w_in_ref[layer]).astype(BF16)
        wb_ref[layer] = (w_back_ref[layer].astype(F32) * 0.5).astype(BF16)

    def rows_of(patch):
        return pl.ds(pl.multiple_of(patch * width, 8), width)

    def pair_of(ref, first):
        return jnp.concatenate([ref[rows_of(first), :], ref[rows_of(first + 1), :]], axis=1)

    def put_pair(ref, first, value):
        ref[rows_of(first), :] = value[:, :lanes]
        ref[rows_of(first + 1), :] = value[:, lanes:]

    def matmul(left, right):
        return jnp.dot(left, right, preferred_element_type=F32)

    slot = lax.broadcasted_iota(jnp.int32, (depth, lanes), 0)
    spot = jnp.where(slot < 8, -1, lax.rem(slot + (part_rows - 8), part_rows))
    eight = lax.broadcasted_iota(jnp.int32, (8, lanes), 0)

    def embed_input(patch):
        top = (patch // half_side) * (2 * side) + lax.rem(patch, half_side) * 2
        block = jnp.zeros((8, lanes), F32)
        for index, offset in enumerate((0, 1, side, side + 1)):
            block = jnp.where(eight == index, spin_ref[pl.ds(top + offset, 1), :], block)
        onehot = (spot == patch).astype(F32)
        return jnp.concatenate([block, onehot[8:]], axis=0).astype(BF16)

    def start(index, carry):
        firsts = [(index * GROUP + member) * 2 for member in range(GROUP)]
        streams = []
        for first in firsts:
            right = jnp.concatenate([embed_input(first), embed_input(first + 1)], axis=1)
            streams.append(matmul(embed_ref[...], right))
        norms = [layer_norm(stream).astype(BF16) for stream in streams]
        values = [matmul(wv_ref[0], norm) for norm in norms]
        for first, stream, value in zip(firsts, streams, values):
            put_pair(x_ref, first, stream)
            put_pair(v_ref, first, value)
        return carry

    lax.fori_loop(0, patch_count // (2 * GROUP), start, 0)
    pool_ref[...] = jnp.zeros(pool_ref.shape, F32)

    for layer in range(layers):
        for head in range(heads):
            places = [
                pl.ds(head * per_head + index, patch_count, stride=width)
                for index in range(per_head)
            ]
            value = jnp.concatenate([v_ref[spot_rows, :] for spot_rows in places], axis=1)
            across = mixing_ref[
                pl.ds(head * patch_count * layers + layer, patch_count, stride=layers), :
            ]
            mixed = matmul(across.astype(BF16), value.astype(BF16))
            for index, spot_rows in enumerate(places):
                v_ref[spot_rows, :] = mixed[:, index * lanes : (index + 1) * lanes]

        def block(index, carry, layer=layer):
            firsts = [(index * GROUP + member) * 2 for member in range(GROUP)]
            olds = [pair_of(x_ref, first) for first in firsts]
            mixes = [pair_of(v_ref, first).astype(BF16) for first in firsts]
            streams = [old + matmul(wo_ref[layer], mix) for old, mix in zip(olds, mixes)]
            norms = [layer_norm(stream).astype(BF16) for stream in streams]
            hiddens = [
                twice_gelu(matmul(wi_ref[layer], norm)).astype(BF16) for norm in norms
            ]
            streams = [
                stream + matmul(wb_ref[layer], hidden)
                for stream, hidden in zip(streams, hiddens)
            ]
            norms = [layer_norm(stream) for stream in streams]
            if layer + 1 < layers:
                values = [matmul(wv_ref[layer + 1], norm.astype(BF16)) for norm in norms]
                for first, stream, value in zip(firsts, streams, values):
                    put_pair(x_ref, first, stream)
                    put_pair(v_ref, first, value)
            else:
                parts = [norm[:, :lanes] + norm[:, lanes:] for norm in norms]
                pool_ref[...] += functools.reduce(jnp.add, parts)
            return carry

        lax.fori_loop(0, patch_count // (2 * GROUP), block, 0)

    pooled = pool_ref[...] / half_side
    bias = jnp.transpose(jnp.broadcast_to(b_final_ref[...], (lanes, width)))
    final = lax.dot_general(
        w_final_ref[...], pooled, (((0,), (0,)), ((), ())),
        preferred_element_type=F32, precision=lax.Precision.HIGHEST,
    ) + bias
    size = jnp.abs(final)
    curve = size + jnp.log1p(jnp.exp(-2.0 * size)) - math.log(2.0)
    amps = jnp.sum(curve, axis=0, keepdims=True) * (1.0 / width)
    for step in range(steps):
        proposal_ref[step : step + 1, :] = amps[:, step * chains : (step + 1) * chains]
    amp_ref[...] = amps[:, steps * chains : (steps + 1) * chains]


def on_device(
    init_up, flip_site, accept, swap_ok, ladder_bit, w_embed, pos_embed, w_value, mixing, w_out,
    w_in, w_back, w_final, b_final,
):
    rungs, groups = lax.axis_size("ladder"), lax.axis_size("grp")
    chains, sites = init_up.shape
    steps = flip_site.shape[0]
    patch_count, width = pos_embed.shape
    layers, hidden_width = w_in.shape[0], w_in.shape[2]
    ups, flips, accepts, counts = exchange(init_up, flip_site, accept, rungs, groups)
    lanes = -(-(steps + 1) * chains // 128) * 128
    rows = -(-(steps + 1) // 8) * 8
    depth = 8 + 3 * (-(-patch_count // 8) * 8)
    proposals, spins, amp, totals = pl.pallas_call(
        window_kernel,
        out_shape=(
            jax.ShapeDtypeStruct((steps, chains), F32),
            jax.ShapeDtypeStruct((chains, sites), F32),
            jax.ShapeDtypeStruct((1, chains), F32),
            jax.ShapeDtypeStruct((1, steps), F32),
        ),
        in_specs=[pl.BlockSpec(memory_space=VMEM)] * 18,
        out_specs=[pl.BlockSpec(memory_space=VMEM)] * 4,
        scratch_shapes=[
            VMEM((rows, lanes), jnp.int32),
            VMEM((sites, lanes), F32),
            VMEM((patch_count * width, lanes), F32),
            VMEM((patch_count * width, lanes), F32),
            VMEM((width, depth), BF16),
            VMEM((layers, width, width), BF16),
            VMEM((layers, width, width), BF16),
            VMEM((layers, hidden_width, width), BF16),
            VMEM((layers, width, hidden_width), BF16),
            VMEM((width, lanes), F32),
        ],
        name="window",
    )(
        init_up, flip_site, accept, ups, flips, accepts, counts, swap_ok, ladder_bit.T, w_embed,
        pos_embed, w_value, mixing.transpose(1, 2, 0, 3).reshape(-1, patch_count), w_out, w_in,
        w_back.swapaxes(1, 2), w_final, b_final.reshape(1, width),
    )
    return proposals, spins, amp.reshape(chains), totals


def solution(mesh):
    placed = (
        P(("ladder", "grp"), None),
        P(None, ("ladder", "grp")),
        P(None, ("ladder", "grp")),
        P(None, None, "grp"),
        P(None, "grp"),
    ) + (P(),) * 9
    return jax.shard_map(
        on_device,
        mesh=mesh,
        in_specs=placed,
        out_specs=(
            P(None, ("ladder", "grp")),
            P(("ladder", "grp"), None),
            P(("ladder", "grp")),
            P("ladder", None),
        ),
        check_vma=False,
    )
```

```python
import functools
import math

import jax
import jax.numpy as jnp
from jax import lax
from jax.experimental import pallas as pl
from jax.experimental.pallas import tpu as pltpu
from jax.sharding import PartitionSpec as P

MESH = pl.DeviceIdType.MESH
VMEM = pltpu.VMEM
F32 = jnp.float32
BF16 = jnp.bfloat16
GROUP = 9


def transposed(matrix):
    wide = matrix.shape[1]
    eye = (
        lax.broadcasted_iota(jnp.int32, (wide, wide), 0)
        == lax.broadcasted_iota(jnp.int32, (wide, wide), 1)
    )
    return lax.dot_general(
        eye.astype(F32).astype(matrix.dtype),
        matrix,
        (((1,), (1,)), ((), ())),
        preferred_element_type=F32,
    )


def layer_norm(values):
    scale = 1.0 / values.shape[0]
    center = values - jnp.sum(values, axis=0, keepdims=True) * scale
    spread = jnp.sum(center * center, axis=0, keepdims=True) * scale
    return center * lax.rsqrt(spread + 1e-05)


def twice_gelu(values):
    root = math.sqrt(2.0 / math.pi)
    inner = values * (root + (root * 0.044715) * (values * values))
    return values + values * jnp.tanh(inner)


def window_kernel(
    rungs, groups, up_ref, flip_ref, accept_ref, swap_ref, bit_ref, w_embed_ref, pos_ref, w_value_ref, mixing_ref, w_out_ref, w_in_ref,
    w_back_ref,
    pool_ref, spins_out_ref, totals_ref,
    event_ref, spin_ref, x_ref, v_ref, embed_ref, wv_ref, wo_ref, wi_ref, wb_ref,
    ups_ref, flips_ref, accepts_ref, counts_ref, send_sem, recv_sem, group_send, group_recv,
):
    chains, sites = up_ref.shape
    steps = flip_ref.shape[0]
    bits = rungs.bit_length() - 1
    patch_count, width = pos_ref.shape
    layers = w_value_ref.shape[0]
    heads = mixing_ref.shape[0] // (layers * patch_count)
    per_head = width // heads
    hidden_width = w_in_ref.shape[2]
    lanes = event_ref.shape[1]
    side = math.isqrt(sites)
    half_side = side // 2
    rung = lax.axis_index("ladder")

    place = lax.axis_index("grp")
    over_ladder = [(jnp.bitwise_xor(rung, apart), place) for apart in range(1, rungs)]
    over_group = [(rung, jnp.bitwise_xor(place, apart)) for apart in range(1, groups)]
    barrier = pltpu.get_barrier_semaphore()
    for device in over_ladder + over_group:
        pl.semaphore_signal(barrier, inc=1, device_id=device, device_id_type=MESH)
    pl.semaphore_wait(barrier, rungs - 1 + groups - 1)
    walkers = [
        pltpu.make_async_remote_copy(
            src_ref=source,
            dst_ref=landing.at[index],
            send_sem=send_sem.at[index, part],
            recv_sem=recv_sem.at[index, part],
            device_id=device,
            device_id_type=MESH,
        )
        for index, device in enumerate(over_ladder)
        for part, (source, landing) in enumerate(
            ((up_ref, ups_ref), (flip_ref, flips_ref), (accept_ref, accepts_ref))
        )
    ]
    tallies = [
        pltpu.make_async_remote_copy(
            src_ref=accept_ref,
            dst_ref=counts_ref.at[index],
            send_sem=group_send.at[index],
            recv_sem=group_recv.at[index],
            device_id=device,
            device_id_type=MESH,
        )
        for index, device in enumerate(over_group)
    ]
    for copy in walkers + tallies:
        copy.start()

    depth = embed_ref.shape[1]
    part_rows = (depth - 8) // 3
    pos = pos_ref[...]
    high = pos.astype(BF16)
    middle = (pos - high.astype(F32)).astype(BF16)
    low = (pos - high.astype(F32) - middle.astype(F32)).astype(BF16)
    blank = jnp.zeros((part_rows - patch_count, width), F32)
    pieces = [w_embed_ref[...].astype(F32), jnp.zeros((8 - w_embed_ref.shape[0], width), F32)]
    for part in (high, middle, low):
        pieces += [part.astype(F32), blank]
    embed_ref[...] = transposed(jnp.concatenate(pieces, axis=0).astype(BF16)).astype(BF16)
    for layer in range(layers):
        wv_ref[layer] = transposed(w_value_ref[layer]).astype(BF16)
        wo_ref[layer] = transposed(w_out_ref[layer]).astype(BF16)
        wi_ref[layer] = transposed(w_in_ref[layer]).astype(BF16)
        wb_ref[layer] = (w_back_ref[layer].astype(F32) * 0.5).astype(BF16)

    for copy in walkers:
        copy.wait()

    rows = event_ref.shape[0]
    row = lax.broadcasted_iota(jnp.int32, (rows, chains), 0)
    state = [jnp.where(row == 0, apart, -1) for apart in range(rungs)]
    event_ref[...] = jnp.full(event_ref.shape, -1, jnp.int32)
    for step in range(steps):
        mine = slice(step, step + 1)
        moved = []
        for apart in range(rungs):
            sites_here = flip_ref[mine, :] if apart == 0 else flips_ref[apart - 1, mine, :]
            taken = accept_ref[mine, :] if apart == 0 else accepts_ref[apart - 1, mine, :]
            if apart == 0:
                event_ref[:, step * chains : (step + 1) * chains] = jnp.where(
                    row == step + 1, sites_here, state[0]
                )
            moved.append(
                jnp.where(row == step + 1, jnp.where(taken == 1, sites_here, -1), state[apart])
            )
        chosen = bit_ref[:, mine]
        after = []
        for apart in range(rungs):
            here = jnp.bitwise_xor(rung, apart)
            value = moved[apart]
            for bit in range(bits):
                mask = 2**bit
                pair = (here // (2 * mask)) * mask + lax.rem(here, mask)
                decided = jnp.where(chosen == bit, swap_ref[step, pl.ds(pair, 1), :], 0)
                value = jnp.where(
                    jnp.broadcast_to(decided, value.shape) == 1, moved[apart ^ mask], value
                )
            after.append(value)
        state = after
    event_ref[:, steps * chains : (steps + 1) * chains] = state[0]

    events = event_ref[...]
    lane = lax.broadcasted_iota(jnp.int32, (1, lanes), 1)
    wanted = events[0:1, :] * chains + lax.rem(lane, chains)
    member = lax.broadcasted_iota(jnp.int32, (rungs * chains, lanes), 0)
    pick = (member == wanted).astype(F32).astype(BF16)
    everyone = jnp.concatenate(
        [up_ref[...], ups_ref[...].reshape((rungs - 1) * chains, sites)], axis=0
    )
    picked = lax.dot_general(
        everyone.astype(F32).astype(BF16), pick, (((0,), (0,)), ((), ())),
        preferred_element_type=F32,
    )
    spins = 2.0 * picked - 1.0
    site = lax.broadcasted_iota(jnp.int32, (sites, lanes), 0)
    for step in range(steps):
        spins = jnp.where(site == events[step + 1 : step + 2, :], -spins, spins)
    spin_ref[...] = spins
    last = (
        lax.broadcasted_iota(jnp.int32, (chains, lanes), 1)
        == lax.broadcasted_iota(jnp.int32, (chains, lanes), 0) + steps * chains
    )
    spins_out_ref[...] = lax.dot_general(
        last.astype(F32).astype(BF16), spins.astype(BF16), (((1,), (1,)), ((), ())),
        preferred_element_type=F32,
    )

    def rows_of(patch):
        return pl.ds(pl.multiple_of(patch * width, 8), width)

    def pair_of(ref, first):
        return jnp.concatenate([ref[rows_of(first), :], ref[rows_of(first + 1), :]], axis=1)

    def put_pair(ref, first, value):
        ref[rows_of(first), :] = value[:, :lanes]
        ref[rows_of(first + 1), :] = value[:, lanes:]

    def matmul(left, right):
        return jnp.dot(left, right, preferred_element_type=F32)

    slot = lax.broadcasted_iota(jnp.int32, (depth, lanes), 0)
    spot = jnp.where(slot < 8, -1, lax.rem(slot + (part_rows - 8), part_rows))
    eight = lax.broadcasted_iota(jnp.int32, (8, lanes), 0)

    def embed_input(patch):
        top = (patch // half_side) * (2 * side) + lax.rem(patch, half_side) * 2
        block = jnp.zeros((8, lanes), F32)
        for index, offset in enumerate((0, 1, side, side + 1)):
            block = jnp.where(eight == index, spin_ref[pl.ds(top + offset, 1), :], block)
        onehot = (spot == patch).astype(F32)
        return jnp.concatenate([block, onehot[8:]], axis=0).astype(BF16)

    def start(index, carry):
        firsts = [(index * GROUP + member) * 2 for member in range(GROUP)]
        streams = []
        for first in firsts:
            right = jnp.concatenate([embed_input(first), embed_input(first + 1)], axis=1)
            streams.append(matmul(embed_ref[...], right))
        norms = [layer_norm(stream).astype(BF16) for stream in streams]
        values = [matmul(wv_ref[0], norm) for norm in norms]
        for first, stream, value in zip(firsts, streams, values):
            put_pair(x_ref, first, stream)
            put_pair(v_ref, first, value)
        return carry

    lax.fori_loop(0, patch_count // (2 * GROUP), start, 0)
    pool_ref[...] = jnp.zeros(pool_ref.shape, F32)

    for layer in range(layers):
        for head in range(heads):
            places = [
                pl.ds(head * per_head + index, patch_count, stride=width)
                for index in range(per_head)
            ]
            value = jnp.concatenate([v_ref[spot_rows, :] for spot_rows in places], axis=1)
            across = mixing_ref[
                pl.ds(head * patch_count * layers + layer, patch_count, stride=layers), :
            ]
            mixed = matmul(across.astype(BF16), value.astype(BF16))
            for index, spot_rows in enumerate(places):
                v_ref[spot_rows, :] = mixed[:, index * lanes : (index + 1) * lanes]

        def block(index, carry, layer=layer):
            firsts = [(index * GROUP + member) * 2 for member in range(GROUP)]
            olds = [pair_of(x_ref, first) for first in firsts]
            mixes = [pair_of(v_ref, first).astype(BF16) for first in firsts]
            streams = [old + matmul(wo_ref[layer], mix) for old, mix in zip(olds, mixes)]
            norms = [layer_norm(stream).astype(BF16) for stream in streams]
            hiddens = [
                twice_gelu(matmul(wi_ref[layer], norm)).astype(BF16) for norm in norms
            ]
            streams = [
                stream + matmul(wb_ref[layer], hidden)
                for stream, hidden in zip(streams, hiddens)
            ]
            norms = [layer_norm(stream) for stream in streams]
            if layer + 1 < layers:
                values = [matmul(wv_ref[layer + 1], norm.astype(BF16)) for norm in norms]
                for first, stream, value in zip(firsts, streams, values):
                    put_pair(x_ref, first, stream)
                    put_pair(v_ref, first, value)
            else:
                parts = [norm[:, :lanes] + norm[:, lanes:] for norm in norms]
                pool_ref[...] += functools.reduce(jnp.add, parts)
            return carry

        lax.fori_loop(0, patch_count // (2 * GROUP), block, 0)

    for copy in tallies:
        copy.wait()
    accepted = accept_ref[...] + jnp.sum(counts_ref[...], axis=0)
    totals_ref[...] = lax.dot_general(
        jnp.ones((1, chains), F32), accepted.astype(F32), (((1,), (1,)), ((), ())),
        preferred_element_type=F32, precision=lax.Precision.HIGHEST,
    )


def head_kernel(
    half_side, pool_ref, spins_ref, totals_ref, w_final_ref, b_final_ref,
    proposal_ref, spins_out_ref, amp_ref, totals_out_ref,
):
    width, lanes = pool_ref.shape
    steps, chains = proposal_ref.shape
    spins_out_ref[...] = spins_ref[...]
    totals_out_ref[...] = totals_ref[...]
    pooled = pool_ref[...] / half_side
    bias = jnp.transpose(jnp.broadcast_to(b_final_ref[...], (lanes, width)))
    final = lax.dot_general(
        w_final_ref[...], pooled, (((0,), (0,)), ((), ())),
        preferred_element_type=F32, precision=lax.Precision.HIGHEST,
    ) + bias
    size = jnp.abs(final)
    curve = size + jnp.log1p(jnp.exp(-2.0 * size)) - math.log(2.0)
    amps = jnp.sum(curve, axis=0, keepdims=True) * (1.0 / width)
    for step in range(steps):
        proposal_ref[step : step + 1, :] = amps[:, step * chains : (step + 1) * chains]
    amp_ref[...] = amps[:, steps * chains : (steps + 1) * chains]


def on_device(
    init_up, flip_site, accept, swap_ok, ladder_bit, w_embed, pos_embed, w_value, mixing, w_out,
    w_in, w_back, w_final, b_final,
):
    rungs, groups = lax.axis_size("ladder"), lax.axis_size("grp")
    chains, sites = init_up.shape
    steps = flip_site.shape[0]
    patch_count, width = pos_embed.shape
    layers, hidden_width = w_in.shape[0], w_in.shape[2]
    lanes = -(-(steps + 1) * chains // 128) * 128
    rows = -(-(steps + 1) // 8) * 8
    depth = 8 + 3 * (-(-patch_count // 8) * 8)
    pool, spins, totals = pl.pallas_call(
        functools.partial(window_kernel, rungs, groups),
        out_shape=(
            jax.ShapeDtypeStruct((width, lanes), F32),
            jax.ShapeDtypeStruct((chains, sites), F32),
            jax.ShapeDtypeStruct((1, steps), F32),
        ),
        in_specs=[pl.BlockSpec(memory_space=VMEM)] * 12,
        out_specs=[pl.BlockSpec(memory_space=VMEM)] * 3,
        scratch_shapes=[
            VMEM((rows, lanes), jnp.int32),
            VMEM((sites, lanes), F32),
            VMEM((patch_count * width, lanes), F32),
            VMEM((patch_count * width, lanes), F32),
            VMEM((width, depth), BF16),
            VMEM((layers, width, width), BF16),
            VMEM((layers, width, width), BF16),
            VMEM((layers, hidden_width, width), BF16),
            VMEM((layers, width, hidden_width), BF16),
            VMEM((rungs - 1,) + init_up.shape, jnp.int32),
            VMEM((rungs - 1,) + flip_site.shape, jnp.int32),
            VMEM((rungs - 1,) + accept.shape, jnp.int32),
            VMEM((groups - 1,) + accept.shape, jnp.int32),
            pltpu.SemaphoreType.DMA((rungs - 1, 3)),
            pltpu.SemaphoreType.DMA((rungs - 1, 3)),
            pltpu.SemaphoreType.DMA((groups - 1,)),
            pltpu.SemaphoreType.DMA((groups - 1,)),
        ],
        compiler_params=pltpu.CompilerParams(collective_id=0, has_side_effects=True),
        name="window",
    )(
        init_up, flip_site, accept, swap_ok, ladder_bit.T, w_embed,
        pos_embed, w_value, mixing.transpose(1, 2, 0, 3).reshape(-1, patch_count), w_out, w_in,
        w_back.swapaxes(1, 2),
    )
    half_side = math.isqrt(sites) // 2
    proposals, spins, amp, totals = pl.pallas_call(
        functools.partial(head_kernel, half_side),
        out_shape=(
            jax.ShapeDtypeStruct((steps, chains), F32),
            jax.ShapeDtypeStruct((chains, sites), F32),
            jax.ShapeDtypeStruct((1, chains), F32),
            jax.ShapeDtypeStruct((1, steps), F32),
        ),
        in_specs=[pl.BlockSpec(memory_space=VMEM)] * 5,
        out_specs=[pl.BlockSpec(memory_space=VMEM)] * 4,
        name="head",
    )(pool, spins, totals, w_final, b_final.reshape(1, width))
    return proposals, spins, amp.reshape(chains), totals


def solution(mesh):
    placed = (
        P(("ladder", "grp"), None),
        P(None, ("ladder", "grp")),
        P(None, ("ladder", "grp")),
        P(None, None, "grp"),
        P(None, "grp"),
    ) + (P(),) * 9
    return jax.shard_map(
        on_device,
        mesh=mesh,
        in_specs=placed,
        out_specs=(
            P(None, ("ladder", "grp")),
            P(("ladder", "grp"), None),
            P(("ladder", "grp")),
            P("ladder", None),
        ),
        check_vma=False,
    )
```

```python
import functools
import math

import jax
import jax.numpy as jnp
from jax import lax
from jax.experimental import pallas as pl
from jax.experimental.pallas import tpu as pltpu
from jax.sharding import PartitionSpec as P

MESH = pl.DeviceIdType.MESH
VMEM = pltpu.VMEM
F32 = jnp.float32
BF16 = jnp.bfloat16
GROUP = 9


def transposed(matrix):
    wide = matrix.shape[1]
    eye = (
        lax.broadcasted_iota(jnp.int32, (wide, wide), 0)
        == lax.broadcasted_iota(jnp.int32, (wide, wide), 1)
    )
    return lax.dot_general(
        eye.astype(F32).astype(matrix.dtype),
        matrix,
        (((1,), (1,)), ((), ())),
        preferred_element_type=F32,
    )


def layer_norm(values):
    scale = 1.0 / values.shape[0]
    center = values - jnp.sum(values, axis=0, keepdims=True) * scale
    spread = jnp.sum(center * center, axis=0, keepdims=True) * scale
    return center * lax.rsqrt(spread + 1e-05)


def twice_gelu(values):
    root = math.sqrt(2.0 / math.pi)
    inner = values * (root + (root * 0.044715) * (values * values))
    return values + values * jnp.tanh(inner)


def window_kernel(
    rungs, groups, up_ref, flip_ref, accept_ref, swap_ref, bit_ref, w_embed_hbm, pos_hbm, w_value_hbm, mixing_hbm, w_out_hbm, w_in_hbm,
    w_back_hbm,
    pool_ref, spins_out_ref, totals_ref,
    event_ref, spin_ref, x_ref, v_ref, embed_ref, wv_ref, wo_ref, wi_ref, wb_ref,
    ups_ref, flips_ref, accepts_ref, counts_ref, send_sem, recv_sem, group_send, group_recv,
    w_embed_ref, pos_ref, w_value_ref, mixing_ref, w_out_ref, w_in_ref, w_back_ref, load_sem,
):
    chains, sites = up_ref.shape
    steps = flip_ref.shape[0]
    bits = rungs.bit_length() - 1
    patch_count, width = pos_ref.shape
    layers = w_value_ref.shape[0]
    heads = mixing_ref.shape[0] // (layers * patch_count)
    per_head = width // heads
    hidden_width = w_in_ref.shape[2]
    lanes = event_ref.shape[1]
    side = math.isqrt(sites)
    half_side = side // 2
    rung = lax.axis_index("ladder")

    place = lax.axis_index("grp")
    over_ladder = [(jnp.bitwise_xor(rung, apart), place) for apart in range(1, rungs)]
    over_group = [(rung, jnp.bitwise_xor(place, apart)) for apart in range(1, groups)]
    barrier = pltpu.get_barrier_semaphore()
    for device in over_ladder + over_group:
        pl.semaphore_signal(barrier, inc=1, device_id=device, device_id_type=MESH)
    loads = [
        pltpu.make_async_copy(source, landing, load_sem.at[index])
        for index, (source, landing) in enumerate(
            (
                (w_embed_hbm, w_embed_ref), (pos_hbm, pos_ref), (w_value_hbm, w_value_ref),
                (w_out_hbm, w_out_ref), (w_in_hbm, w_in_ref), (w_back_hbm, w_back_ref),
                (mixing_hbm, mixing_ref),
            )
        )
    ]
    for load in loads:
        load.start()
    pl.semaphore_wait(barrier, rungs - 1 + groups - 1)
    walkers = [
        pltpu.make_async_remote_copy(
            src_ref=source,
            dst_ref=landing.at[index],
            send_sem=send_sem.at[index, part],
            recv_sem=recv_sem.at[index, part],
            device_id=device,
            device_id_type=MESH,
        )
        for index, device in enumerate(over_ladder)
        for part, (source, landing) in enumerate(
            ((up_ref, ups_ref), (flip_ref, flips_ref), (accept_ref, accepts_ref))
        )
    ]
    tallies = [
        pltpu.make_async_remote_copy(
            src_ref=accept_ref,
            dst_ref=counts_ref.at[index],
            send_sem=group_send.at[index],
            recv_sem=group_recv.at[index],
            device_id=device,
            device_id_type=MESH,
        )
        for index, device in enumerate(over_group)
    ]
    for copy in walkers + tallies:
        copy.start()

    for load in loads:
        load.wait()

    depth = embed_ref.shape[1]
    part_rows = (depth - 8) // 3
    pos = pos_ref[...]
    high = pos.astype(BF16)
    middle = (pos - high.astype(F32)).astype(BF16)
    low = (pos - high.astype(F32) - middle.astype(F32)).astype(BF16)
    blank = jnp.zeros((part_rows - patch_count, width), F32)
    pieces = [w_embed_ref[...].astype(F32), jnp.zeros((8 - w_embed_ref.shape[0], width), F32)]
    for part in (high, middle, low):
        pieces += [part.astype(F32), blank]
    embed_ref[...] = transposed(jnp.concatenate(pieces, axis=0).astype(BF16)).astype(BF16)
    for layer in range(layers):
        wv_ref[layer] = transposed(w_value_ref[layer]).astype(BF16)
        wo_ref[layer] = transposed(w_out_ref[layer]).astype(BF16)
        wi_ref[layer] = transposed(w_in_ref[layer]).astype(BF16)
        wb_ref[layer] = (w_back_ref[layer].astype(F32) * 0.5).astype(BF16)

    for copy in walkers:
        copy.wait()

    rows = event_ref.shape[0]
    row = lax.broadcasted_iota(jnp.int32, (rows, chains), 0)
    state = [jnp.where(row == 0, apart, -1) for apart in range(rungs)]
    event_ref[...] = jnp.full(event_ref.shape, -1, jnp.int32)
    for step in range(steps):
        mine = slice(step, step + 1)
        moved = []
        for apart in range(rungs):
            sites_here = flip_ref[mine, :] if apart == 0 else flips_ref[apart - 1, mine, :]
            taken = accept_ref[mine, :] if apart == 0 else accepts_ref[apart - 1, mine, :]
            if apart == 0:
                event_ref[:, step * chains : (step + 1) * chains] = jnp.where(
                    row == step + 1, sites_here, state[0]
                )
            moved.append(
                jnp.where(row == step + 1, jnp.where(taken == 1, sites_here, -1), state[apart])
            )
        chosen = bit_ref[:, mine]
        after = []
        for apart in range(rungs):
            here = jnp.bitwise_xor(rung, apart)
            value = moved[apart]
            for bit in range(bits):
                mask = 2**bit
                pair = (here // (2 * mask)) * mask + lax.rem(here, mask)
                decided = jnp.where(chosen == bit, swap_ref[step, pl.ds(pair, 1), :], 0)
                value = jnp.where(
                    jnp.broadcast_to(decided, value.shape) == 1, moved[apart ^ mask], value
                )
            after.append(value)
        state = after
    event_ref[:, steps * chains : (steps + 1) * chains] = state[0]

    events = event_ref[...]
    lane = lax.broadcasted_iota(jnp.int32, (1, lanes), 1)
    wanted = events[0:1, :] * chains + lax.rem(lane, chains)
    member = lax.broadcasted_iota(jnp.int32, (rungs * chains, lanes), 0)
    pick = (member == wanted).astype(F32).astype(BF16)
    everyone = jnp.concatenate(
        [up_ref[...], ups_ref[...].reshape((rungs - 1) * chains, sites)], axis=0
    )
    picked = lax.dot_general(
        everyone.astype(F32).astype(BF16), pick, (((0,), (0,)), ((), ())),
        preferred_element_type=F32,
    )
    spins = 2.0 * picked - 1.0
    site = lax.broadcasted_iota(jnp.int32, (sites, lanes), 0)
    for step in range(steps):
        spins = jnp.where(site == events[step + 1 : step + 2, :], -spins, spins)
    spin_ref[...] = spins
    last = (
        lax.broadcasted_iota(jnp.int32, (chains, lanes), 1)
        == lax.broadcasted_iota(jnp.int32, (chains, lanes), 0) + steps * chains
    )
    spins_out_ref[...] = lax.dot_general(
        last.astype(F32).astype(BF16), spins.astype(BF16), (((1,), (1,)), ((), ())),
        preferred_element_type=F32,
    )

    def rows_of(patch):
        return pl.ds(pl.multiple_of(patch * width, 8), width)

    def pair_of(ref, first):
        return jnp.concatenate([ref[rows_of(first), :], ref[rows_of(first + 1), :]], axis=1)

    def put_pair(ref, first, value):
        ref[rows_of(first), :] = value[:, :lanes]
        ref[rows_of(first + 1), :] = value[:, lanes:]

    def matmul(left, right):
        return jnp.dot(left, right, preferred_element_type=F32)

    slot = lax.broadcasted_iota(jnp.int32, (depth, lanes), 0)
    spot = jnp.where(slot < 8, -1, lax.rem(slot + (part_rows - 8), part_rows))
    eight = lax.broadcasted_iota(jnp.int32, (8, lanes), 0)

    def embed_input(patch):
        top = (patch // half_side) * (2 * side) + lax.rem(patch, half_side) * 2
        block = jnp.zeros((8, lanes), F32)
        for index, offset in enumerate((0, 1, side, side + 1)):
            block = jnp.where(eight == index, spin_ref[pl.ds(top + offset, 1), :], block)
        onehot = (spot == patch).astype(F32)
        return jnp.concatenate([block, onehot[8:]], axis=0).astype(BF16)

    def start(index, carry):
        firsts = [(index * GROUP + member) * 2 for member in range(GROUP)]
        streams = []
        for first in firsts:
            right = jnp.concatenate([embed_input(first), embed_input(first + 1)], axis=1)
            streams.append(matmul(embed_ref[...], right))
        norms = [layer_norm(stream).astype(BF16) for stream in streams]
        values = [matmul(wv_ref[0], norm) for norm in norms]
        for first, stream, value in zip(firsts, streams, values):
            put_pair(x_ref, first, stream)
            put_pair(v_ref, first, value)
        return carry

    lax.fori_loop(0, patch_count // (2 * GROUP), start, 0)
    pool_ref[...] = jnp.zeros(pool_ref.shape, F32)

    for layer in range(layers):
        for head in range(heads):
            places = [
                pl.ds(head * per_head + index, patch_count, stride=width)
                for index in range(per_head)
            ]
            value = jnp.concatenate([v_ref[spot_rows, :] for spot_rows in places], axis=1)
            across = mixing_ref[
                pl.ds(head * patch_count * layers + layer, patch_count, stride=layers), :
            ]
            mixed = matmul(across.astype(BF16), value.astype(BF16))
            for index, spot_rows in enumerate(places):
                v_ref[spot_rows, :] = mixed[:, index * lanes : (index + 1) * lanes]

        def block(index, carry, layer=layer):
            firsts = [(index * GROUP + member) * 2 for member in range(GROUP)]
            olds = [pair_of(x_ref, first) for first in firsts]
            mixes = [pair_of(v_ref, first).astype(BF16) for first in firsts]
            streams = [old + matmul(wo_ref[layer], mix) for old, mix in zip(olds, mixes)]
            norms = [layer_norm(stream).astype(BF16) for stream in streams]
            hiddens = [
                twice_gelu(matmul(wi_ref[layer], norm).astype(BF16)) for norm in norms
            ]
            streams = [
                stream + matmul(wb_ref[layer], hidden)
                for stream, hidden in zip(streams, hiddens)
            ]
            norms = [layer_norm(stream) for stream in streams]
            if layer + 1 < layers:
                values = [matmul(wv_ref[layer + 1], norm.astype(BF16)) for norm in norms]
                for first, stream, value in zip(firsts, streams, values):
                    put_pair(x_ref, first, stream)
                    put_pair(v_ref, first, value)
            else:
                parts = [norm[:, :lanes] + norm[:, lanes:] for norm in norms]
                pool_ref[...] += functools.reduce(jnp.add, parts)
            return carry

        lax.fori_loop(0, patch_count // (2 * GROUP), block, 0)

    for copy in tallies:
        copy.wait()
    accepted = accept_ref[...] + jnp.sum(counts_ref[...], axis=0)
    totals_ref[...] = lax.dot_general(
        jnp.ones((1, chains), F32), accepted.astype(F32), (((1,), (1,)), ((), ())),
        preferred_element_type=F32, precision=lax.Precision.HIGHEST,
    )


def head_kernel(
    half_side, pool_ref, spins_ref, totals_ref, w_final_ref, b_final_ref,
    proposal_ref, spins_out_ref, amp_ref, totals_out_ref,
):
    width, lanes = pool_ref.shape
    steps, chains = proposal_ref.shape
    spins_out_ref[...] = spins_ref[...]
    totals_out_ref[...] = totals_ref[...]
    pooled = pool_ref[...] / half_side
    bias = jnp.transpose(jnp.broadcast_to(b_final_ref[...], (lanes, width)))
    final = lax.dot_general(
        w_final_ref[...], pooled, (((0,), (0,)), ((), ())),
        preferred_element_type=F32, precision=lax.Precision.HIGHEST,
    ) + bias
    size = jnp.abs(final)
    curve = size + jnp.log1p(jnp.exp(-2.0 * size)) - math.log(2.0)
    amps = jnp.sum(curve, axis=0, keepdims=True) * (1.0 / width)
    for step in range(steps):
        proposal_ref[step : step + 1, :] = amps[:, step * chains : (step + 1) * chains]
    amp_ref[...] = amps[:, steps * chains : (steps + 1) * chains]


def on_device(
    init_up, flip_site, accept, swap_ok, ladder_bit, w_embed, pos_embed, w_value, mixing, w_out,
    w_in, w_back, w_final, b_final,
):
    rungs, groups = lax.axis_size("ladder"), lax.axis_size("grp")
    chains, sites = init_up.shape
    steps = flip_site.shape[0]
    patch_count, width = pos_embed.shape
    layers, hidden_width = w_in.shape[0], w_in.shape[2]
    lanes = -(-(steps + 1) * chains // 128) * 128
    rows = -(-(steps + 1) // 8) * 8
    depth = 8 + 3 * (-(-patch_count // 8) * 8)
    weights = (
        w_embed, pos_embed, w_value,
        mixing.transpose(1, 2, 0, 3).reshape(-1, patch_count), w_out, w_in,
        w_back.swapaxes(1, 2),
    )
    pool, spins, totals = pl.pallas_call(
        functools.partial(window_kernel, rungs, groups),
        out_shape=(
            jax.ShapeDtypeStruct((width, lanes), F32),
            jax.ShapeDtypeStruct((chains, sites), F32),
            jax.ShapeDtypeStruct((1, steps), F32),
        ),
        in_specs=[pl.BlockSpec(memory_space=VMEM)] * 5
        + [pl.BlockSpec(memory_space=pl.ANY)] * len(weights),
        out_specs=[pl.BlockSpec(memory_space=VMEM)] * 3,
        scratch_shapes=[
            VMEM((rows, lanes), jnp.int32),
            VMEM((sites, lanes), F32),
            VMEM((patch_count * width, lanes), F32),
            VMEM((patch_count * width, lanes), F32),
            VMEM((width, depth), BF16),
            VMEM((layers, width, width), BF16),
            VMEM((layers, width, width), BF16),
            VMEM((layers, hidden_width, width), BF16),
            VMEM((layers, width, hidden_width), BF16),
            VMEM((rungs - 1,) + init_up.shape, jnp.int32),
            VMEM((rungs - 1,) + flip_site.shape, jnp.int32),
            VMEM((rungs - 1,) + accept.shape, jnp.int32),
            VMEM((groups - 1,) + accept.shape, jnp.int32),
            pltpu.SemaphoreType.DMA((rungs - 1, 3)),
            pltpu.SemaphoreType.DMA((rungs - 1, 3)),
            pltpu.SemaphoreType.DMA((groups - 1,)),
            pltpu.SemaphoreType.DMA((groups - 1,)),
        ]
        + [VMEM(weight.shape, weight.dtype) for weight in weights]
        + [pltpu.SemaphoreType.DMA((len(weights),))],
        compiler_params=pltpu.CompilerParams(collective_id=0, has_side_effects=True),
        name="window",
    )(
        init_up, flip_site, accept, swap_ok, ladder_bit.T, *weights
    )
    half_side = math.isqrt(sites) // 2
    proposals, spins, amp, totals = pl.pallas_call(
        functools.partial(head_kernel, half_side),
        out_shape=(
            jax.ShapeDtypeStruct((steps, chains), F32),
            jax.ShapeDtypeStruct((chains, sites), F32),
            jax.ShapeDtypeStruct((1, chains), F32),
            jax.ShapeDtypeStruct((1, steps), F32),
        ),
        in_specs=[pl.BlockSpec(memory_space=VMEM)] * 5,
        out_specs=[pl.BlockSpec(memory_space=VMEM)] * 4,
        name="head",
    )(pool, spins, totals, w_final, b_final.reshape(1, width))
    return proposals, spins, amp.reshape(chains), totals


def solution(mesh):
    placed = (
        P(("ladder", "grp"), None),
        P(None, ("ladder", "grp")),
        P(None, ("ladder", "grp")),
        P(None, None, "grp"),
        P(None, "grp"),
    ) + (P(),) * 9
    return jax.shard_map(
        on_device,
        mesh=mesh,
        in_specs=placed,
        out_specs=(
            P(None, ("ladder", "grp")),
            P(("ladder", "grp"), None),
            P(("ladder", "grp")),
            P("ladder", None),
        ),
        check_vma=False,
    )
```

```python
import functools
import math

import jax
import jax.numpy as jnp
from jax import lax
from jax.experimental import pallas as pl
from jax.experimental.pallas import tpu as pltpu
from jax.sharding import PartitionSpec as P

MESH = pl.DeviceIdType.MESH
VMEM = pltpu.VMEM
F32 = jnp.float32
BF16 = jnp.bfloat16
GROUP = 9


def transposed(matrix):
    wide = matrix.shape[1]
    eye = (
        lax.broadcasted_iota(jnp.int32, (wide, wide), 0)
        == lax.broadcasted_iota(jnp.int32, (wide, wide), 1)
    )
    return lax.dot_general(
        eye.astype(F32).astype(matrix.dtype),
        matrix,
        (((1,), (1,)), ((), ())),
        preferred_element_type=F32,
    )


def layer_norm(values):
    scale = 1.0 / values.shape[0]
    center = values - jnp.sum(values, axis=0, keepdims=True) * scale
    spread = jnp.sum(center * center, axis=0, keepdims=True) * scale
    return center * lax.rsqrt(spread + 1e-05)


def twice_gelu(values):
    root = math.sqrt(2.0 / math.pi)
    inner = values * (root + (root * 0.044715) * (values * values))
    return values + values * jnp.tanh(inner)


def window_kernel(
    rungs, groups, up_ref, flip_ref, accept_ref, swap_ref, bit_ref, w_embed_hbm, pos_hbm, w_value_hbm, mixing_hbm, w_out_hbm, w_in_hbm,
    w_back_hbm,
    pool_ref, spins_out_ref, totals_ref,
    event_ref, spin_ref, x_ref, v_ref, embed_ref, wv_ref, wo_ref, wi_ref, wb_ref,
    ups_ref, flips_ref, accepts_ref, counts_ref, send_sem, recv_sem, group_send, group_recv,
    w_embed_ref, pos_ref, w_value_ref, mixing_ref, w_out_ref, w_in_ref, w_back_ref, load_sem,
):
    chains, sites = up_ref.shape
    steps = flip_ref.shape[0]
    bits = rungs.bit_length() - 1
    patch_count, width = pos_ref.shape
    layers = w_value_ref.shape[0]
    heads = mixing_hbm.shape[0] // (layers * patch_count)
    per_head = width // heads
    hidden_width = w_in_ref.shape[2]
    lanes = event_ref.shape[1]
    side = math.isqrt(sites)
    half_side = side // 2
    rung = lax.axis_index("ladder")

    place = lax.axis_index("grp")
    over_ladder = [(jnp.bitwise_xor(rung, apart), place) for apart in range(1, rungs)]
    over_group = [(rung, jnp.bitwise_xor(place, apart)) for apart in range(1, groups)]
    barrier = pltpu.get_barrier_semaphore()
    for device in over_ladder + over_group:
        pl.semaphore_signal(barrier, inc=1, device_id=device, device_id_type=MESH)
    loads = [
        pltpu.make_async_copy(source, landing, load_sem.at[index])
        for index, (source, landing) in enumerate(
            (
                (w_embed_hbm, w_embed_ref), (pos_hbm, pos_ref), (w_value_hbm, w_value_ref),
                (w_out_hbm, w_out_ref), (w_in_hbm, w_in_ref), (w_back_hbm, w_back_ref),
                (mixing_hbm, mixing_ref.at[pl.ds(0, mixing_hbm.shape[0])]),
            )
        )
    ]
    for load in loads:
        load.start()
    pl.semaphore_wait(barrier, rungs - 1 + groups - 1)
    walkers = [
        pltpu.make_async_remote_copy(
            src_ref=source,
            dst_ref=landing.at[index],
            send_sem=send_sem.at[index, part],
            recv_sem=recv_sem.at[index, part],
            device_id=device,
            device_id_type=MESH,
        )
        for index, device in enumerate(over_ladder)
        for part, (source, landing) in enumerate(
            ((up_ref, ups_ref), (flip_ref, flips_ref), (accept_ref, accepts_ref))
        )
    ]
    tallies = [
        pltpu.make_async_remote_copy(
            src_ref=accept_ref,
            dst_ref=counts_ref.at[index],
            send_sem=group_send.at[index],
            recv_sem=group_recv.at[index],
            device_id=device,
            device_id_type=MESH,
        )
        for index, device in enumerate(over_group)
    ]
    for copy in walkers + tallies:
        copy.start()

    for load in loads:
        load.wait()

    depth = embed_ref.shape[1]
    part_rows = (depth - 8) // 3
    pos = pos_ref[...]
    high = pos.astype(BF16)
    middle = (pos - high.astype(F32)).astype(BF16)
    low = (pos - high.astype(F32) - middle.astype(F32)).astype(BF16)
    blank = jnp.zeros((part_rows - patch_count, width), F32)
    pieces = [w_embed_ref[...].astype(F32), jnp.zeros((8 - w_embed_ref.shape[0], width), F32)]
    for part in (high, middle, low):
        pieces += [part.astype(F32), blank]
    embed_ref[...] = transposed(jnp.concatenate(pieces, axis=0).astype(BF16)).astype(BF16)
    for layer in range(layers):
        wv_ref[layer] = transposed(w_value_ref[layer]).astype(BF16)
        wo_ref[layer] = transposed(w_out_ref[layer]).astype(BF16)
        wi_ref[layer] = transposed(w_in_ref[layer]).astype(BF16)
        wb_ref[layer] = (w_back_ref[layer].astype(F32) * 0.5).astype(BF16)

    for copy in walkers:
        copy.wait()

    rows = event_ref.shape[0]
    row = lax.broadcasted_iota(jnp.int32, (rows, chains), 0)
    state = [jnp.where(row == 0, apart, -1) for apart in range(rungs)]
    event_ref[...] = jnp.full(event_ref.shape, -1, jnp.int32)
    for step in range(steps):
        mine = slice(step, step + 1)
        moved = []
        for apart in range(rungs):
            sites_here = flip_ref[mine, :] if apart == 0 else flips_ref[apart - 1, mine, :]
            taken = accept_ref[mine, :] if apart == 0 else accepts_ref[apart - 1, mine, :]
            if apart == 0:
                event_ref[:, step * chains : (step + 1) * chains] = jnp.where(
                    row == step + 1, sites_here, state[0]
                )
            moved.append(
                jnp.where(row == step + 1, jnp.where(taken == 1, sites_here, -1), state[apart])
            )
        chosen = bit_ref[:, mine]
        after = []
        for apart in range(rungs):
            here = jnp.bitwise_xor(rung, apart)
            value = moved[apart]
            for bit in range(bits):
                mask = 2**bit
                pair = (here // (2 * mask)) * mask + lax.rem(here, mask)
                decided = jnp.where(chosen == bit, swap_ref[step, pl.ds(pair, 1), :], 0)
                value = jnp.where(
                    jnp.broadcast_to(decided, value.shape) == 1, moved[apart ^ mask], value
                )
            after.append(value)
        state = after
    event_ref[:, steps * chains : (steps + 1) * chains] = state[0]

    events = event_ref[...]
    lane = lax.broadcasted_iota(jnp.int32, (1, lanes), 1)
    wanted = events[0:1, :] * chains + lax.rem(lane, chains)
    member = lax.broadcasted_iota(jnp.int32, (rungs * chains, lanes), 0)
    pick = (member == wanted).astype(F32).astype(BF16)
    everyone = jnp.concatenate(
        [up_ref[...], ups_ref[...].reshape((rungs - 1) * chains, sites)], axis=0
    )
    picked = lax.dot_general(
        everyone.astype(F32).astype(BF16), pick, (((0,), (0,)), ((), ())),
        preferred_element_type=F32,
    )
    spins = 2.0 * picked - 1.0
    site = lax.broadcasted_iota(jnp.int32, (sites, lanes), 0)
    for step in range(steps):
        spins = jnp.where(site == events[step + 1 : step + 2, :], -spins, spins)
    spin_ref[...] = spins
    last = (
        lax.broadcasted_iota(jnp.int32, (chains, lanes), 1)
        == lax.broadcasted_iota(jnp.int32, (chains, lanes), 0) + steps * chains
    )
    spins_out_ref[...] = lax.dot_general(
        last.astype(F32).astype(BF16), spins.astype(BF16), (((1,), (1,)), ((), ())),
        preferred_element_type=F32,
    )

    def rows_of(patch):
        return pl.ds(pl.multiple_of(patch * width, 8), width)

    def pair_of(ref, first):
        return jnp.concatenate([ref[rows_of(first), :], ref[rows_of(first + 1), :]], axis=1)

    def put_pair(ref, first, value):
        ref[rows_of(first), :] = value[:, :lanes]
        ref[rows_of(first + 1), :] = value[:, lanes:]

    def matmul(left, right):
        return jnp.dot(left, right, preferred_element_type=F32)

    slot = lax.broadcasted_iota(jnp.int32, (depth, lanes), 0)
    spot = jnp.where(slot < 8, -1, lax.rem(slot + (part_rows - 8), part_rows))
    eight = lax.broadcasted_iota(jnp.int32, (8, lanes), 0)

    def embed_input(patch):
        top = (patch // half_side) * (2 * side) + lax.rem(patch, half_side) * 2
        block = jnp.zeros((8, lanes), F32)
        for index, offset in enumerate((0, 1, side, side + 1)):
            block = jnp.where(eight == index, spin_ref[pl.ds(top + offset, 1), :], block)
        onehot = (spot == patch).astype(F32)
        return jnp.concatenate([block, onehot[8:]], axis=0).astype(BF16)

    def start(index, carry):
        firsts = [(index * GROUP + member) * 2 for member in range(GROUP)]
        streams = []
        for first in firsts:
            right = jnp.concatenate([embed_input(first), embed_input(first + 1)], axis=1)
            streams.append(matmul(embed_ref[...], right))
        norms = [layer_norm(stream).astype(BF16) for stream in streams]
        values = [matmul(wv_ref[0], norm) for norm in norms]
        for first, stream, value in zip(firsts, streams, values):
            put_pair(x_ref, first, stream)
            put_pair(v_ref, first, value)
        return carry

    lax.fori_loop(0, patch_count // (2 * GROUP), start, 0)
    pool_ref[...] = jnp.zeros(pool_ref.shape, F32)

    for layer in range(layers):
        for head in range(heads):
            places = [
                pl.ds(head * per_head + index, patch_count, stride=width)
                for index in range(per_head)
            ]
            value = jnp.concatenate([v_ref[spot_rows, :] for spot_rows in places], axis=1)
            across = mixing_ref[
                pl.ds(head * patch_count * layers + layer, patch_count, stride=layers), :
            ]
            mixed = matmul(across.astype(BF16), value.astype(BF16))
            for index, spot_rows in enumerate(places):
                v_ref[spot_rows, :] = mixed[:, index * lanes : (index + 1) * lanes]

        def block(index, carry, layer=layer):
            firsts = [(index * GROUP + member) * 2 for member in range(GROUP)]
            olds = [pair_of(x_ref, first) for first in firsts]
            mixes = [pair_of(v_ref, first).astype(BF16) for first in firsts]
            streams = [old + matmul(wo_ref[layer], mix) for old, mix in zip(olds, mixes)]
            norms = [layer_norm(stream).astype(BF16) for stream in streams]
            hiddens = [
                twice_gelu(matmul(wi_ref[layer], norm).astype(BF16)) for norm in norms
            ]
            streams = [
                stream + matmul(wb_ref[layer], hidden)
                for stream, hidden in zip(streams, hiddens)
            ]
            norms = [layer_norm(stream) for stream in streams]
            if layer + 1 < layers:
                values = [matmul(wv_ref[layer + 1], norm.astype(BF16)) for norm in norms]
                for first, stream, value in zip(firsts, streams, values):
                    put_pair(x_ref, first, stream)
                    put_pair(v_ref, first, value)
            else:
                parts = [norm[:, :lanes] + norm[:, lanes:] for norm in norms]
                pool_ref[...] += functools.reduce(jnp.add, parts)
            return carry

        lax.fori_loop(0, patch_count // (2 * GROUP), block, 0)

    for copy in tallies:
        copy.wait()
    accepted = accept_ref[...] + jnp.sum(counts_ref[...], axis=0)
    totals_ref[...] = lax.dot_general(
        jnp.ones((1, chains), F32), accepted.astype(F32), (((1,), (1,)), ((), ())),
        preferred_element_type=F32, precision=lax.Precision.HIGHEST,
    )


def head_kernel(
    half_side, pool_ref, spins_ref, totals_ref, w_final_ref, b_final_ref,
    proposal_ref, spins_out_ref, amp_ref, totals_out_ref,
):
    width, lanes = pool_ref.shape
    steps, chains = proposal_ref.shape
    spins_out_ref[...] = spins_ref[...]
    totals_out_ref[...] = totals_ref[...]
    pooled = pool_ref[...] / half_side
    bias = jnp.transpose(jnp.broadcast_to(b_final_ref[...], (lanes, width)))
    final = lax.dot_general(
        w_final_ref[...], pooled, (((0,), (0,)), ((), ())),
        preferred_element_type=F32, precision=lax.Precision.HIGHEST,
    ) + bias
    size = jnp.abs(final)
    curve = size + jnp.log1p(jnp.exp(-2.0 * size)) - math.log(2.0)
    amps = jnp.sum(curve, axis=0, keepdims=True) * (1.0 / width)
    for step in range(steps):
        proposal_ref[step : step + 1, :] = amps[:, step * chains : (step + 1) * chains]
    amp_ref[...] = amps[:, steps * chains : (steps + 1) * chains]


def on_device(
    init_up, flip_site, accept, swap_ok, ladder_bit, w_embed, pos_embed, w_value, mixing, w_out,
    w_in, w_back, w_final, b_final,
):
    rungs, groups = lax.axis_size("ladder"), lax.axis_size("grp")
    chains, sites = init_up.shape
    steps = flip_site.shape[0]
    patch_count, width = pos_embed.shape
    layers, hidden_width = w_in.shape[0], w_in.shape[2]
    lanes = -(-(steps + 1) * chains // 128) * 128
    rows = -(-(steps + 1) // 8) * 8
    depth = 8 + 3 * (-(-patch_count // 8) * 8)
    weights = (
        w_embed, pos_embed, w_value,
        mixing.transpose(1, 2, 0, 3).reshape(-1, patch_count), w_out, w_in,
        w_back.swapaxes(1, 2),
    )
    pool, spins, totals = pl.pallas_call(
        functools.partial(window_kernel, rungs, groups),
        out_shape=(
            jax.ShapeDtypeStruct((width, lanes), F32),
            jax.ShapeDtypeStruct((chains, sites), F32),
            jax.ShapeDtypeStruct((1, steps), F32),
        ),
        in_specs=[pl.BlockSpec(memory_space=VMEM)] * 5
        + [pl.BlockSpec(memory_space=pl.ANY)] * len(weights),
        out_specs=[pl.BlockSpec(memory_space=VMEM)] * 3,
        scratch_shapes=[
            VMEM((rows, lanes), jnp.int32),
            VMEM((sites, lanes), F32),
            VMEM((patch_count * width, lanes), F32),
            VMEM((-(-patch_count // 8) * 8 * width, lanes), F32),
            VMEM((width, depth), BF16),
            VMEM((layers, width, width), BF16),
            VMEM((layers, width, width), BF16),
            VMEM((layers, hidden_width, width), BF16),
            VMEM((layers, width, hidden_width), BF16),
            VMEM((rungs - 1,) + init_up.shape, jnp.int32),
            VMEM((rungs - 1,) + flip_site.shape, jnp.int32),
            VMEM((rungs - 1,) + accept.shape, jnp.int32),
            VMEM((groups - 1,) + accept.shape, jnp.int32),
            pltpu.SemaphoreType.DMA((rungs - 1, 3)),
            pltpu.SemaphoreType.DMA((rungs - 1, 3)),
            pltpu.SemaphoreType.DMA((groups - 1,)),
            pltpu.SemaphoreType.DMA((groups - 1,)),
        ]
        + [VMEM(weight.shape, weight.dtype) for weight in weights[:3]]
        + [VMEM((weights[3].shape[0] + 8 * layers, patch_count), F32)]
        + [VMEM(weight.shape, weight.dtype) for weight in weights[4:]]
        + [pltpu.SemaphoreType.DMA((len(weights),))],
        compiler_params=pltpu.CompilerParams(collective_id=0, has_side_effects=True),
        name="window",
    )(
        init_up, flip_site, accept, swap_ok, ladder_bit.T, *weights
    )
    half_side = math.isqrt(sites) // 2
    proposals, spins, amp, totals = pl.pallas_call(
        functools.partial(head_kernel, half_side),
        out_shape=(
            jax.ShapeDtypeStruct((steps, chains), F32),
            jax.ShapeDtypeStruct((chains, sites), F32),
            jax.ShapeDtypeStruct((1, chains), F32),
            jax.ShapeDtypeStruct((1, steps), F32),
        ),
        in_specs=[pl.BlockSpec(memory_space=VMEM)] * 5,
        out_specs=[pl.BlockSpec(memory_space=VMEM)] * 4,
        name="head",
    )(pool, spins, totals, w_final, b_final.reshape(1, width))
    return proposals, spins, amp.reshape(chains), totals


def solution(mesh):
    placed = (
        P(("ladder", "grp"), None),
        P(None, ("ladder", "grp")),
        P(None, ("ladder", "grp")),
        P(None, None, "grp"),
        P(None, "grp"),
    ) + (P(),) * 9
    return jax.shard_map(
        on_device,
        mesh=mesh,
        in_specs=placed,
        out_specs=(
            P(None, ("ladder", "grp")),
            P(("ladder", "grp"), None),
            P(("ladder", "grp")),
            P("ladder", None),
        ),
        check_vma=False,
    )
```
